32 devices in a mesh: rows: 8 (over z, x), cols: 4 (over y, core).
Axes of the slice: x: 2, y: 2, z: 4, core: 2. Of those that a mesh axis runs over, the one named last changes fastest.
Arguments:
- points: float32 [16, 32768], P(None, ('rows', 'cols')), may hold values from -6 to 6
- lengthscales: float32 [16], replicated, may hold values from 2 to 3
- targets: float32 [64, 32768], P(None, ('rows', 'cols')), may hold values from -6 to 6
- inducing_weights: bfloat16 [64, 2048], P(None, 'cols'), may hold values from -0.59765625 to 0.59765625
- inducing_index: int32 [2048], replicated, may hold values from 0 to 32767
- block_order: int32 [3], replicated, may hold values from 0 to 31
- block_inverse: bfloat16 [32, 1024, 1024], P(('rows', 'cols')), may hold values from -0.1 to 0.1
Outputs:
- residual: float32 [64, 32768], P(None, ('rows', 'cols'))
- weights: float32 [64, 32768], P(None, ('rows', 'cols'))
The draws below stay inside these ranges and needn't reach their ends.
All inputs are finite; a program needn't handle non-finite values.
Results may differ from the reference program's by a relative error of at most 0.00095.
The reference program's roundings to bfloat16 on the way count: a program that leaves them out, or rounds other values in their place, can miss the bound.
Values may be sent and summed in bfloat16 or wider, within the bound.
No kernel may reach another device: no remote copies, remote signals or barrier semaphores. Data moves between devices by JAX's collectives and lax.ppermute only.
A program may use at most 64 MiB of HBM per device.

```python
import math
import jax
import jax.numpy as jnp
from jax import lax

DIM = 16
COLS = 64
INDUCING = 2048
BLK = 1024
PTS_DEV = 1024
STEPS = 3
NPTS = 32768
BLOCKS = 32


def draw_points(key, part):
    point_key = jax.random.fold_in(key, 29)
    values = jnp.clip(1.5 * jax.random.normal(point_key, (DIM, NPTS), jnp.float32), -6.0, 6.0)
    return values


def draw_block_inverse(key, part):
    first_key, second_key = jax.random.split(jax.random.fold_in(key, 17))
    diagonal = jnp.exp(jax.random.uniform(first_key, (BLOCKS, BLK), jnp.float32, math.log(0.03), math.log(0.099)))
    offdiag = jnp.clip(jax.random.normal(second_key, (BLOCKS, BLK, BLK), jnp.float32), -4.0, 4.0)
    offdiag = offdiag * (0.012 / math.sqrt(BLK))
    identity = jnp.eye(BLK, dtype=jnp.float32)
    return (offdiag * (1.0 - identity) + diagonal[:, :, None] * identity).astype(jnp.bfloat16)


def place_ends(array, key, least, largest):
    longest = array.shape.index(max(array.shape))
    spots = []
    for shift in (0, 1):
        where = [jax.random.randint(jax.random.fold_in(key, axis), (), 0, length) for axis, length in enumerate(array.shape)]
        where[longest] = (where[longest] + shift) % array.shape[longest]
        spots.append(tuple(where))
    return array.at[spots[0]].set(least).at[spots[1]].set(largest)


def levels(rng, dims, shards, smallest, largest):
    def one(dim, blocks):
        steps = jax.random.uniform(jax.random.fold_in(jax.random.fold_in(rng, 6), dim), (blocks,), jnp.float32, smallest / len(shards), largest / len(shards))
        return jnp.repeat(jnp.exp(steps), dims[dim] // blocks).reshape((-1,) + (1,) * (len(dims) - dim - 1))

    factor_of = one(*shards[0])
    for cut in shards[1:]:
        factor_of = factor_of * one(*cut)
    return factor_of


def bell_draw(own_key, extent, spread, bound, shards=(), held_as=jnp.bfloat16):
    entries = spread * jax.random.normal(own_key, extent, jnp.float32)
    if shards:
        entries = entries * levels(own_key, extent, shards, -0.22, 0.18)
    return jnp.clip(entries, -bound, bound).astype(held_as)


def setup_inputs(seed: int = 0) -> dict:
    splits = jax.random.split(jax.random.key(seed), 8)
    points = draw_points(jax.random.fold_in(splits[7], 71), 0)
    lengthscales = jnp.clip(jnp.exp(jax.random.uniform(splits[1], (DIM,), jnp.float32, math.log(2.0), math.log(3.0))), 2.0, 3.0)
    targets = bell_draw(splits[2], (COLS, NPTS), 1.0, 6.0, ((1, 32),), jnp.float32)
    inducing_weights = bell_draw(splits[3], (COLS, INDUCING), 0.1, 0.59765625, ((1, 4),))
    inducing_index = place_ends(jax.random.randint(splits[4], (INDUCING,), 0, NPTS), jax.random.fold_in(splits[4], 1), 0, NPTS - 1).astype(jnp.int32)
    block_order = jax.random.randint(splits[5], (STEPS,), 0, BLOCKS).astype(jnp.int32)
    block_inverse = draw_block_inverse(jax.random.fold_in(splits[7], 71), 0)
    return {"points": points, "lengthscales": lengthscales, "targets": targets, "inducing_weights": inducing_weights, "inducing_index": inducing_index, "block_order": block_order, "block_inverse": block_inverse}


noise_var = 0.5


def kernel_tile(left, right):
    crossed = lax.dot_general(left, right, (((0,), (0,)), ((), ())), precision=lax.Precision.HIGHEST, preferred_element_type=jnp.float32)
    left_sq = jnp.sum(left * left, axis=0)
    right_sq = jnp.sum(right * right, axis=0)
    return jnp.exp(-0.5 * (left_sq[:, None] + right_sq[None, :] - 2.0 * crossed)).astype(jnp.bfloat16)


def reference(points, lengthscales, targets, inducing_weights, inducing_index, block_order, block_inverse):
    scaled = points / lengthscales[:, None]
    anchors = jnp.take(scaled, inducing_index, axis=1)
    slab_count = NPTS // PTS_DEV

    def warm_slab(slab_no):
        coords = lax.dynamic_slice_in_dim(scaled, slab_no * PTS_DEV, PTS_DEV, 1)
        return jnp.dot(inducing_weights, kernel_tile(anchors, coords), preferred_element_type=jnp.float32)

    predicted = lax.map(warm_slab, jnp.arange(slab_count, dtype=jnp.int32))
    predicted = jnp.transpose(predicted, (1, 0, 2)).reshape(COLS, NPTS)
    residual = targets - predicted
    weights = jnp.zeros((COLS, NPTS), jnp.float32)
    for step_no in range(STEPS):
        block_id = block_order[step_no]
        offset = (block_id * BLK).astype(jnp.int32)
        shifted = lax.dynamic_slice_in_dim(residual, offset, BLK, 1).astype(jnp.bfloat16)
        delta = jnp.dot(shifted, block_inverse[block_id], preferred_element_type=jnp.float32).astype(jnp.bfloat16)
        block_coords = lax.dynamic_slice_in_dim(scaled, offset, BLK, 1)

        def step_slab(slab_no):
            coords = lax.dynamic_slice_in_dim(scaled, slab_no * PTS_DEV, PTS_DEV, 1)
            return jnp.dot(delta, kernel_tile(block_coords, coords), preferred_element_type=jnp.float32)

        updates = lax.map(step_slab, jnp.arange(slab_count, dtype=jnp.int32))
        residual = residual - jnp.transpose(updates, (1, 0, 2)).reshape(COLS, NPTS)
        delta_f = delta.astype(jnp.float32)
        block_res = lax.dynamic_slice_in_dim(residual, offset, BLK, 1)
        residual = lax.dynamic_update_slice_in_dim(residual, block_res - noise_var * delta_f, offset, 1)
        block_wts = lax.dynamic_slice_in_dim(weights, offset, BLK, 1)
        weights = lax.dynamic_update_slice_in_dim(weights, block_wts + delta_f, offset, 1)
    return residual, weights
```

```python
import math

import jax
import jax.numpy as jnp
from jax import lax
from jax.sharding import PartitionSpec as P

noise_var = 0.5
ALL = ("rows", "cols")
LANES = 128


def exchange(value, mask):
    count = lax.axis_size(ALL)
    return lax.ppermute(value, ALL, [(i, i ^ mask) for i in range(count)])


def mask_groups():
    count = lax.axis_size(ALL)
    bits = [1 << k for k in range(1, count.bit_length() - 1)]
    return [bits[k : k + 2] for k in range(0, len(bits), 2)]


def spread_step(candidate, owner_id):
    device_id = lax.axis_index(ALL)
    core = device_id & 1
    half = candidate.shape[0] // 2
    mine = lax.dynamic_slice_in_dim(candidate, core * half, half, 0)
    other = lax.dynamic_slice_in_dim(candidate, (1 - core) * half, half, 0)
    away = device_id ^ owner_id
    held = jnp.where((away & 1) == 0, mine, exchange(other, 1))
    for bits in mask_groups():
        masks = [bits[0]] if len(bits) == 1 else [bits[0], bits[1], bits[0] | bits[1]]
        near = away & sum(bits)
        arrived = [exchange(held, mask) for mask in masks]
        for mask, value in zip(masks, arrived):
            held = jnp.where(near == mask, value, held)
    partner = exchange(held, 1)
    low = jnp.where(core == 0, held, partner)
    high = jnp.where(core == 0, partner, held)
    return jnp.concatenate([low, high], axis=0)


def to_tiles(value):
    rows, columns = value.shape
    return (
        value.reshape(rows // 4, 4, columns // LANES, LANES)
        .transpose(0, 2, 1, 3)
        .reshape(-1, 4, LANES)
    )


def from_tiles(tiles, rows):
    columns = tiles.shape[0] * 4 * LANES // rows
    return (
        tiles.reshape(rows // 4, columns // LANES, 4, LANES)
        .transpose(0, 2, 1, 3)
        .reshape(rows, columns)
    )


def share_inputs(masked, scaled, owners):
    count = lax.axis_size(ALL)
    steps = owners.shape[0]
    dims = scaled.shape[0]
    anchor_tiles, block_tiles = to_tiles(masked), to_tiles(scaled)
    n_anchor, n_block = anchor_tiles.shape[0], block_tiles.shape[0]
    per_anchor, per_block = -(-n_anchor // count), -(-n_block // count)

    def padded(tiles, per):
        extra = per * count - tiles.shape[0]
        return jnp.pad(tiles, ((0, extra), (0, 0), (0, 0))).reshape(count, per, 4, LANES)

    out = jnp.concatenate(
        [padded(anchor_tiles, per_anchor), padded(block_tiles, per_block)], axis=1
    )
    per = per_anchor + per_block
    got = lax.all_to_all(out.reshape(count * per, 4, LANES), ALL, 0, 0, tiled=True)
    got = got.reshape(count, per, 4, LANES)
    total = jnp.sum(got[:, :per_anchor], axis=0)
    picked = [
        lax.dynamic_index_in_dim(got[:, per_anchor:], owners[k], 0, keepdims=False)
        for k in range(steps)
    ]
    piece = jnp.concatenate([total, *picked], axis=0)
    per = piece.shape[0]
    spread = jnp.broadcast_to(piece[None], (count, per, 4, LANES)).reshape(count * per, 4, LANES)
    got = lax.all_to_all(spread, ALL, 0, 0, tiled=True).reshape(count, per, 4, LANES)
    anchors = from_tiles(got[:, :per_anchor].reshape(-1, 4, LANES)[:n_anchor], dims)
    blocks = []
    for k in range(steps):
        first = per_anchor + k * per_block
        tiles = got[:, first : first + per_block].reshape(-1, 4, LANES)[:n_block]
        blocks.append(from_tiles(tiles, dims))
    return anchors, blocks


def kernel_tile(left, right):
    crossed = lax.dot_general(
        left,
        right,
        (((0,), (0,)), ((), ())),
        precision=lax.Precision.HIGHEST,
        preferred_element_type=jnp.float32,
    )
    left_sq = jnp.sum(left * left, axis=0)
    right_sq = jnp.sum(right * right, axis=0)
    return jnp.exp(-0.5 * (left_sq[:, None] + right_sq[None, :] - 2.0 * crossed)).astype(
        jnp.bfloat16
    )


def body(
    points, lengthscales, targets, inducing_weights, inducing_index, block_order, block_inverse
):
    points_dev = points.shape[1]
    per_device = block_inverse.shape[0]
    step_count = block_order.shape[0]
    device_id = lax.axis_index(ALL)
    scaled = points / lengthscales[:, None]
    owners = block_order // per_device
    slots = block_order % per_device
    local_index = inducing_index - device_id * points_dev
    inside = (local_index >= 0) & (local_index < points_dev)
    picked = jnp.take(scaled, jnp.clip(local_index, 0, points_dev - 1), axis=1)
    masked = jnp.where(inside[None, :], picked, 0.0)
    anchors, blocks = share_inputs(masked, scaled, owners)
    weights_all = lax.all_gather(inducing_weights, "cols", axis=1, tiled=True)
    predicted = jnp.dot(
        weights_all, kernel_tile(anchors, scaled), preferred_element_type=jnp.float32
    )
    residual = targets - predicted
    weights = jnp.zeros_like(residual)
    for step_no in range(step_count):
        owner_id = owners[step_no]
        shifted = residual.astype(jnp.bfloat16)
        candidate = jnp.dot(
            shifted, block_inverse[slots[step_no]], preferred_element_type=jnp.float32
        ).astype(jnp.bfloat16)
        delta = spread_step(candidate, owner_id)
        residual = residual - jnp.dot(
            delta, kernel_tile(blocks[step_no], scaled), preferred_element_type=jnp.float32
        )
        delta_f = delta.astype(jnp.float32)
        is_owner = owner_id == device_id
        residual = jnp.where(is_owner, residual - noise_var * delta_f, residual)
        weights = jnp.where(is_owner, weights + delta_f, weights)
    return (residual, weights)


def solution(mesh):
    placed = (
        P(None, ALL),
        P(),
        P(None, ALL),
        P(None, "cols"),
        P(),
        P(),
        P(ALL, None, None),
    )
    return jax.shard_map(
        body,
        mesh=mesh,
        in_specs=placed,
        out_specs=(P(None, ALL), P(None, ALL)),
        check_vma=False,
    )
```

```python
import functools

import jax
import jax.numpy as jnp
from jax import lax
from jax.experimental import pallas as pl
from jax.experimental.pallas import tpu as pltpu
from jax.sharding import PartitionSpec as P

noise_var = 0.5
ALL = ("rows", "cols")
LANES = 128
UNIT = 4
PACK = 16
CHUNK = 512
WIDE = 256


def exchange(value, mask):
    count = lax.axis_size(ALL)
    return lax.ppermute(value, ALL, [(i, i ^ mask) for i in range(count)])


def mask_groups():
    count = lax.axis_size(ALL)
    bits = [1 << k for k in range(1, count.bit_length() - 1)]
    return [bits[k : k + 2] for k in range(0, len(bits), 2)]


def spread_step(candidate, owner_id):
    device_id = lax.axis_index(ALL)
    core = device_id & 1
    half = candidate.shape[0] // 2
    mine = lax.dynamic_slice_in_dim(candidate, core * half, half, 0)
    other = lax.dynamic_slice_in_dim(candidate, (1 - core) * half, half, 0)
    away = device_id ^ owner_id
    held = jnp.where((away & 1) == 0, mine, exchange(other, 1))
    for bits in mask_groups():
        masks = [bits[0]] if len(bits) == 1 else [bits[0], bits[1], bits[0] | bits[1]]
        near = away & sum(bits)
        arrived = [exchange(held, mask) for mask in masks]
        for mask, value in zip(masks, arrived):
            held = jnp.where(near == mask, value, held)
    partner = exchange(held, 1)
    low = jnp.where(core == 0, held, partner)
    high = jnp.where(core == 0, partner, held)
    return jnp.concatenate([low, high], axis=0)


def split3(value):
    high = value.astype(jnp.bfloat16)
    rest = value - high.astype(jnp.float32)
    middle = rest.astype(jnp.bfloat16)
    low = (rest - middle.astype(jnp.float32)).astype(jnp.bfloat16)
    return high, middle, low


def norm_rows(value, first):
    half = -0.5 * jnp.sum(value * value, axis=0, keepdims=True)
    row = lax.broadcasted_iota(jnp.int32, (PACK, value.shape[1]), 0)
    block = jnp.where(row < 6, 1.0, 0.0)
    for k, part in enumerate(split3(half)):
        block = jnp.where(row == first + k, part.astype(jnp.float32), block)
    return block.astype(jnp.bfloat16)


def pack_left(value):
    high, middle, low = split3(value)
    rows = [high, high, middle, high, low, middle, norm_rows(value, 0), jnp.zeros_like(high)]
    return jnp.concatenate(rows, axis=0)


def pack_right(value):
    high, middle, low = split3(value)
    rows = [high, middle, high, low, high, middle, norm_rows(value, 3), jnp.zeros_like(high)]
    return jnp.concatenate(rows, axis=0)


def kernel_values(left, right):
    exponent = jnp.dot(left, right, preferred_element_type=jnp.float32)
    return jnp.exp(exponent).astype(jnp.bfloat16)


def units_of(rows, columns):
    return [(r, c) for r in range(0, rows, UNIT) for c in range(0, columns, LANES)]


def pick_kernel(per_anchor, base_ref, index_ref, points_ref, scale_ref, out_ref, scaled_ref):
    dims, points = points_ref.shape
    same = lax.broadcasted_iota(jnp.int32, (dims, dims), 0) == lax.broadcasted_iota(
        jnp.int32, (dims, dims), 1
    )
    scale = jnp.sum(jnp.where(same, scale_ref[...], 0.0), axis=1, keepdims=True)
    scaled = points_ref[...] / scale
    scaled_ref[...] = scaled
    count, per = out_ref.shape[:2]
    per_block = per - per_anchor
    anchors = index_ref.shape[1]
    anchor_units, block_units = units_of(dims, anchors), units_of(dims, points)
    if len(anchor_units) < count * per_anchor or len(block_units) < count * per_block:
        out_ref[...] = jnp.zeros_like(out_ref)
    for i, (r, c) in enumerate(block_units):
        out_ref[i // per_block, per_anchor + i % per_block] = scaled[r : r + UNIT, c : c + LANES]
    parts = jnp.concatenate(split3(scaled), axis=0)
    width = min(WIDE, anchors)
    place = {spot: i for i, spot in enumerate(anchor_units)}
    for start in range(0, anchors, width):
        local = index_ref[:, start : start + width] - base_ref[0]
        hot = lax.broadcasted_iota(jnp.int32, (points, width), 0) == local
        got = jnp.dot(parts, hot.astype(jnp.bfloat16), preferred_element_type=jnp.float32)
        got = (got[:dims] + got[dims : 2 * dims]) + got[2 * dims :]
        for r in range(0, dims, UNIT):
            for c in range(0, width, LANES):
                i = place[r, start + c]
                out_ref[i // per_anchor, i % per_anchor] = got[r : r + UNIT, c : c + LANES]


def merge_kernel(per_anchor, owners_ref, got_ref, out_ref):
    count, per = got_ref.shape[:2]
    per_block = per - per_anchor
    total = got_ref[0, :per_anchor]
    for source in range(1, count):
        total = total + got_ref[source, :per_anchor]
    pieces = [total]
    for k in range(owners_ref.shape[0]):
        pieces.append(got_ref[owners_ref[k], per_anchor : per_anchor + per_block])
    piece = jnp.concatenate(pieces, axis=0)
    for target in range(count):
        out_ref[target] = piece


def gather_units(got_ref, first, per, whole_ref):
    for i, (r, c) in enumerate(units_of(*whole_ref.shape)):
        whole_ref[r : r + UNIT, c : c + LANES] = got_ref[i // per, first + i % per]


def warm_kernel(per_anchor, column_ref, got_ref, scaled_ref, *refs):
    *weights, targets_ref, out_ref, anchors_ref = refs
    gather_units(got_ref, 0, per_anchor, anchors_ref)
    right = pack_right(scaled_ref[...])
    total = jnp.zeros(out_ref.shape, jnp.float32)
    share = weights[0].shape[1]
    step = min(CHUNK, share)
    for mask, weights_ref in enumerate(weights):
        origin = (column_ref[0] ^ mask) * share
        for start in range(0, share, step):
            spot = pl.ds(pl.multiple_of(origin + start, LANES), step)
            left = pack_left(anchors_ref[:, spot]).T
            parts = []
            for c in range(0, right.shape[1], WIDE):
                values = kernel_values(left, right[:, c : c + WIDE])
                parts.append(
                    jnp.dot(
                        weights_ref[:, start : start + step],
                        values,
                        preferred_element_type=jnp.float32,
                    )
                )
            total = total + jnp.concatenate(parts, axis=1)
    out_ref[...] = targets_ref[...] - total


def tile_kernel(first, per_block, got_ref, scaled_ref, out_ref, block_ref):
    gather_units(got_ref, first, per_block, block_ref)
    right = pack_right(scaled_ref[...])
    for r in range(0, out_ref.shape[0], WIDE):
        left = pack_left(block_ref[:, r : r + WIDE]).T
        out_ref[r : r + WIDE] = kernel_values(left, right)


def call(kernel, out_shape, scalars, arrays, scratch, flops):
    memory = [pltpu.SMEM] * len(scalars) + [pltpu.VMEM] * len(arrays)
    return pl.pallas_call(
        kernel,
        out_shape=out_shape,
        in_specs=[pl.BlockSpec(memory_space=space) for space in memory],
        out_specs=jax.tree.map(lambda _: pl.BlockSpec(memory_space=pltpu.VMEM), out_shape),
        scratch_shapes=scratch,
        cost_estimate=pl.CostEstimate(flops=flops, transcendentals=0, bytes_accessed=1 << 20),
    )(*scalars, *arrays)


def body(
    points, lengthscales, targets, inducing_weights, inducing_index, block_order, block_inverse
):
    dims, points_dev = points.shape
    per_device = block_inverse.shape[0]
    step_count = block_order.shape[0]
    anchor_count = inducing_index.shape[0]
    count, col_count = lax.axis_size(ALL), lax.axis_size("cols")
    device_id = lax.axis_index(ALL)
    owners = block_order // per_device
    slots = block_order % per_device
    weights_of = [inducing_weights] + [
        lax.ppermute(inducing_weights, "cols", [(i, i ^ mask) for i in range(col_count)])
        for mask in range(1, col_count)
    ]
    per_anchor = -(-len(units_of(dims, anchor_count)) // count)
    per_block = -(-len(units_of(dims, points_dev)) // count)
    tiles = functools.partial(jax.ShapeDtypeStruct, dtype=jnp.float32)
    out, scaled = call(
        functools.partial(pick_kernel, per_anchor),
        (tiles((count, per_anchor + per_block, UNIT, LANES)), tiles(points.shape)),
        [(device_id * points_dev).reshape(1)],
        [inducing_index[None, :], points, lengthscales[None, :]],
        [],
        2 * 3 * dims * points_dev * anchor_count,
    )
    got = lax.all_to_all(out, ALL, 0, 0)
    spread = call(
        functools.partial(merge_kernel, per_anchor),
        tiles((count, per_anchor + step_count * per_block, UNIT, LANES)),
        [owners],
        [got],
        [],
        1 << 20,
    )
    got = lax.all_to_all(spread, ALL, 0, 0)
    residual = call(
        functools.partial(warm_kernel, per_anchor),
        tiles(targets.shape),
        [lax.axis_index("cols").reshape(1)],
        [got, scaled, *weights_of, targets],
        [pltpu.VMEM((dims, anchor_count), jnp.float32)],
        1 << 32,
    )
    weights = jnp.zeros_like(residual)
    for step_no in range(step_count):
        owner_id = owners[step_no]
        shifted = residual.astype(jnp.bfloat16)
        candidate = jnp.dot(
            shifted, block_inverse[slots[step_no]], preferred_element_type=jnp.float32
        ).astype(jnp.bfloat16)
        delta = spread_step(candidate, owner_id)
        tile = call(
            functools.partial(tile_kernel, per_anchor + step_no * per_block, per_block),
            jax.ShapeDtypeStruct((points_dev, points_dev), jnp.bfloat16),
            [],
            [got, scaled],
            [pltpu.VMEM(points.shape, jnp.float32)],
            1 << 31,
        )
        residual = residual - jnp.dot(delta, tile, preferred_element_type=jnp.float32)
        delta_f = delta.astype(jnp.float32)
        is_owner = owner_id == device_id
        residual = jnp.where(is_owner, residual - noise_var * delta_f, residual)
        weights = jnp.where(is_owner, weights + delta_f, weights)
    return (residual, weights)


def solution(mesh):
    placed = (
        P(None, ALL),
        P(),
        P(None, ALL),
        P(None, "cols"),
        P(),
        P(),
        P(ALL, None, None),
    )
    return jax.shard_map(
        body,
        mesh=mesh,
        in_specs=placed,
        out_specs=(P(None, ALL), P(None, ALL)),
        check_vma=False,
    )
```

```python
import functools
import operator

import jax
import jax.numpy as jnp
from jax import lax
from jax.experimental import pallas as pl
from jax.experimental.pallas import tpu as pltpu
from jax.sharding import PartitionSpec as P


noise_var = 0.5
ALL = ("rows", "cols")
LANES = 128
UNIT = 4
PACK = 16
CHUNK = 512
WIDE = 256
LOG2_E = 1.4426950408889634
GRANT = 8 << 20


def exchange(value, mask):
    count = lax.axis_size(ALL)
    return lax.ppermute(value, ALL, [(i, i ^ mask) for i in range(count)])


def mask_groups():
    count = lax.axis_size(ALL)
    bits = [1 << k for k in range(1, count.bit_length() - 1)]
    return [bits[k : k + 2] for k in range(0, len(bits), 2)]


def choose_kernel(step_no, masks, device_ref, owners_ref, *refs):
    *options, out_ref = refs
    near = (device_ref[0] ^ owners_ref[step_no]) & functools.reduce(operator.or_, masks)
    for mask, option_ref in zip(masks, options):

        @pl.when(near == mask)
        def _():
            out_ref[...] = option_ref[...]


def spread_step(mine, other, step_no, device, owners):
    def choose(masks, options):
        (chosen,) = call(
            functools.partial(choose_kernel, step_no, tuple(masks)),
            [on_chip(mine.shape, mine.dtype)],
            [device, owners],
            options,
            [],
            1 << 10,
        )
        return chosen

    held = choose([0, 1], [mine, exchange(other, 1)])
    groups = mask_groups()
    for bits in groups:
        masks = [bits[0]] if len(bits) == 1 else [bits[0], bits[1], bits[0] | bits[1]]
        arrived = []
        for mask in masks:
            arrived.append(exchange(held, mask))
        held = choose([0, *masks], [held, *arrived])
    return held, exchange(held, 1)


def split3(value):
    high = value.astype(jnp.bfloat16)
    rest = value - high.astype(jnp.float32)
    middle = rest.astype(jnp.bfloat16)
    low = (rest - middle.astype(jnp.float32)).astype(jnp.bfloat16)
    return high, middle, low


def norm_rows(value, first):
    half = (-0.5 * LOG2_E) * jnp.sum(value * value, axis=0, keepdims=True)
    row = lax.broadcasted_iota(jnp.int32, (PACK, value.shape[1]), 0)
    block = jnp.where(row < 6, 1.0, 0.0)
    for k, part in enumerate(split3(half)):
        block = jnp.where(row == first + k, part.astype(jnp.float32), block)
    return block.astype(jnp.bfloat16)


def pack_left(value):
    high, middle, low = split3(value * LOG2_E)
    rows = [high, high, middle, high, low, middle, norm_rows(value, 0), jnp.zeros_like(high)]
    return jnp.concatenate(rows, axis=0)


def pack_right(value):
    high, middle, low = split3(value)
    rows = [high, middle, high, low, high, middle, norm_rows(value, 3), jnp.zeros_like(high)]
    return jnp.concatenate(rows, axis=0)


def kernel_values(left, right):
    exponent = jnp.dot(left, right, preferred_element_type=jnp.float32)
    return jnp.exp2(exponent).astype(jnp.bfloat16)


def units_of(rows, columns):
    return [(r, c) for r in range(0, rows, UNIT) for c in range(0, columns, LANES)]


def pick_kernel(per_anchor, device_ref, index_ref, points_ref, scale_ref, out_ref, scaled_ref):
    dims, points = points_ref.shape
    same = lax.broadcasted_iota(jnp.int32, (dims, dims), 0) == lax.broadcasted_iota(
        jnp.int32, (dims, dims), 1
    )
    scale = jnp.sum(jnp.where(same, scale_ref[...], 0.0), axis=1, keepdims=True)
    scaled = points_ref[...] / scale
    scaled_ref[...] = scaled
    count, per = out_ref.shape[:2]
    per_block = per - per_anchor
    anchors = index_ref.shape[1]
    anchor_units, block_units = units_of(dims, anchors), units_of(dims, points)
    if len(anchor_units) < count * per_anchor or len(block_units) < count * per_block:
        out_ref[...] = jnp.zeros_like(out_ref)
    for i, (r, c) in enumerate(block_units):
        out_ref[i // per_block, per_anchor + i % per_block] = scaled[r : r + UNIT, c : c + LANES]
    parts = jnp.concatenate(split3(scaled), axis=0)
    width = min(WIDE, anchors)
    place = {spot: i for i, spot in enumerate(anchor_units)}
    for start in range(0, anchors, width):
        local = index_ref[:, start : start + width] - device_ref[0] * points
        hot = lax.broadcasted_iota(jnp.int32, (points, width), 0) == local
        got = jnp.dot(parts, hot.astype(jnp.bfloat16), preferred_element_type=jnp.float32)
        got = (got[:dims] + got[dims : 2 * dims]) + got[2 * dims :]
        for r in range(0, dims, UNIT):
            for c in range(0, width, LANES):
                i = place[r, start + c]
                out_ref[i // per_anchor, i % per_anchor] = got[r : r + UNIT, c : c + LANES]


def merge_kernel(per_anchor, owners_ref, got_ref, out_ref):
    count, per = got_ref.shape[:2]
    per_block = per - per_anchor
    total = got_ref[0, :per_anchor]
    for source in range(1, count):
        total = total + got_ref[source, :per_anchor]
    pieces = [total]
    for k in range(owners_ref.shape[0]):
        pieces.append(got_ref[owners_ref[k], per_anchor : per_anchor + per_block])
    piece = jnp.concatenate(pieces, axis=0)
    for target in range(count):
        out_ref[target] = piece


def gather_units(got_ref, first, per, whole_ref):
    for i, (r, c) in enumerate(units_of(*whole_ref.shape)):
        whole_ref[r : r + UNIT, c : c + LANES] = got_ref[i // per, first + i % per]


def project(residual, slot, core, inverse_ref, whole_ref, mine_ref, other_ref):
    inverse = inverse_ref[slot]
    product = jnp.dot(residual.astype(jnp.bfloat16), inverse, preferred_element_type=jnp.float32)
    whole_ref[...] = product.astype(jnp.bfloat16)
    half = mine_ref.shape[0]
    mine_ref[...] = whole_ref[pl.ds(pl.multiple_of(core * half, half), half)]
    other_ref[...] = whole_ref[pl.ds(pl.multiple_of((1 - core) * half, half), half)]


def warm_kernel(per_anchor, device_ref, slots_ref, got_ref, scaled_ref, *refs):
    *weights, targets_ref, inverse_ref = refs[:-6]
    out_ref, mine_ref, other_ref, anchors_ref, left_ref, whole_ref = refs[-6:]
    gather_units(got_ref, 0, per_anchor, anchors_ref)
    left_ref[...] = pack_left(anchors_ref[...]).T
    right = pack_right(scaled_ref[...])
    column = lax.rem(device_ref[0], len(weights))
    share = weights[0].shape[1]
    step = min(CHUNK, share)
    for c in range(0, right.shape[1], WIDE):
        total = jnp.zeros((out_ref.shape[0], WIDE), jnp.float32)
        for mask, weights_ref in enumerate(weights):
            origin = (column ^ mask) * share
            for start in range(0, share, step):
                left = left_ref[pl.ds(pl.multiple_of(origin + start, LANES), step)]
                total = total + jnp.dot(
                    weights_ref[:, start : start + step],
                    kernel_values(left, right[:, c : c + WIDE]),
                    preferred_element_type=jnp.float32,
                )
        out_ref[:, c : c + WIDE] = targets_ref[:, c : c + WIDE] - total
    project(out_ref[...], slots_ref[0], device_ref[0] & 1, inverse_ref, whole_ref, mine_ref, other_ref)


def tile_kernel(first, per_block, got_ref, scaled_ref, out_ref, block_ref, left_ref):
    gather_units(got_ref, first, per_block, block_ref)
    left_ref[...] = pack_left(block_ref[...]).T
    right = pack_right(scaled_ref[...])
    for r in range(0, out_ref.shape[0], WIDE):
        for c in range(0, out_ref.shape[1], WIDE):
            out_ref[r : r + WIDE, c : c + WIDE] = kernel_values(
                left_ref[r : r + WIDE], right[:, c : c + WIDE]
            )


def update_kernel(step_no, last, device_ref, owners_ref, slots_ref, held_ref, partner_ref, tile_ref, *refs):
    half = held_ref.shape[0]
    core = device_ref[0] & 1
    if last:
        residual_ref, weights_ref, out_ref, sum_ref, whole_ref = refs
    else:
        residual_ref, weights_ref, inverse_ref = refs[:3]
        out_ref, sum_ref, mine_ref, other_ref, whole_ref = refs[3:]
    whole_ref[pl.ds(pl.multiple_of(core * half, half), half)] = held_ref[...]
    whole_ref[pl.ds(pl.multiple_of((1 - core) * half, half), half)] = partner_ref[...]
    delta = whole_ref[...]
    residual = residual_ref[...] - jnp.dot(
        delta, tile_ref[...], preferred_element_type=jnp.float32
    )
    owned = jnp.where(owners_ref[step_no] == device_ref[0], delta.astype(jnp.float32), 0.0)
    residual = residual - noise_var * owned
    out_ref[...] = residual
    sum_ref[...] = weights_ref[...] + owned
    if not last:
        project(residual, slots_ref[step_no + 1], core, inverse_ref, whole_ref, mine_ref, other_ref)


def on_chip(shape, dtype):
    return pltpu.VMEM(shape, dtype)


def call(kernel, out_shape, scalars, arrays, scratch, flops):
    memory = [pltpu.SMEM] * len(scalars) + [pltpu.VMEM] * len(arrays)
    return pl.pallas_call(
        kernel,
        out_shape=out_shape,
        in_specs=[pl.BlockSpec(memory_space=space) for space in memory],
        out_specs=[pl.BlockSpec(memory_space=pltpu.VMEM) for _ in out_shape],
        scratch_shapes=scratch,
        cost_estimate=pl.CostEstimate(flops=flops, transcendentals=0, bytes_accessed=1 << 20),
        compiler_params=pltpu.CompilerParams(vmem_limit_bytes=GRANT),
    )(*scalars, *[pltpu.with_memory_space_constraint(array, pltpu.VMEM) for array in arrays])


def body(
    points, lengthscales, targets, inducing_weights, inducing_index, block_order, block_inverse
):
    dims, points_dev = points.shape
    per_device = block_inverse.shape[0]
    step_count = block_order.shape[0]
    anchor_count = inducing_index.shape[0]
    count, col_count = lax.axis_size(ALL), lax.axis_size("cols")
    device = lax.axis_index(ALL).reshape(1)
    owners = block_order // per_device
    slots = block_order % per_device
    weights_of = [inducing_weights] + [
        lax.ppermute(inducing_weights, "cols", [(i, i ^ mask) for i in range(col_count)])
        for mask in range(1, col_count)
    ]
    per_anchor = -(-len(units_of(dims, anchor_count)) // count)
    per_block = -(-len(units_of(dims, points_dev)) // count)
    tile_flops = 2 * LANES * points_dev
    half = (targets.shape[0] // 2, points_dev)
    halves = [on_chip(half, jnp.bfloat16)] * 2
    out, scaled = call(
        functools.partial(pick_kernel, per_anchor),
        [
            on_chip((count, per_anchor + per_block, UNIT, LANES), jnp.float32),
            on_chip(points.shape, jnp.float32),
        ],
        [device],
        [inducing_index[None, :], points, lengthscales[None, :]],
        [],
        2 * 3 * dims * points_dev * anchor_count,
    )
    got = lax.all_to_all(out, ALL, 0, 0)
    (spread,) = call(
        functools.partial(merge_kernel, per_anchor),
        [on_chip((count, per_anchor + step_count * per_block, UNIT, LANES), jnp.float32)],
        [owners],
        [got],
        [],
        1 << 20,
    )
    got = lax.all_to_all(spread, ALL, 0, 0)
    residual, mine, other = call(
        functools.partial(warm_kernel, per_anchor),
        [on_chip(targets.shape, jnp.float32), *halves],
        [device, slots],
        [got, scaled, *weights_of, targets, block_inverse],
        [
            pltpu.VMEM((dims, anchor_count), jnp.float32),
            pltpu.VMEM((anchor_count, LANES), jnp.bfloat16),
            pltpu.VMEM(targets.shape, jnp.bfloat16),
        ],
        tile_flops * anchor_count,
    )
    weights = jnp.zeros_like(residual)
    for step_no in range(step_count):
        last = step_no == step_count - 1
        held, partner = spread_step(mine, other, step_no, device, owners)
        (tile,) = call(
            functools.partial(tile_kernel, per_anchor + step_no * per_block, per_block),
            [on_chip((points_dev, points_dev), jnp.bfloat16)],
            [],
            [got, scaled],
            [pltpu.VMEM(points.shape, jnp.float32), pltpu.VMEM((points_dev, LANES), jnp.bfloat16)],
            tile_flops * points_dev,
        )
        state = [held, partner, tile, residual, weights]
        shape = jax.ShapeDtypeStruct if last else on_chip
        results = call(
            functools.partial(update_kernel, step_no, last),
            [shape(targets.shape, jnp.float32)] * 2 + ([] if last else halves),
            [device, owners, slots],
            state if last else state + [block_inverse],
            [pltpu.VMEM(targets.shape, jnp.bfloat16)],
            tile_flops * points_dev // 4,
        )
        residual, weights = results[:2]
        mine, other = results[2:] if not last else (None, None)
    return (residual, weights)


def solution(mesh):
    placed = (
        P(None, ALL),
        P(),
        P(None, ALL),
        P(None, "cols"),
        P(),
        P(),
        P(ALL, None, None),
    )

    return jax.shard_map(
        body,
        mesh=mesh,
        in_specs=placed,
        out_specs=(P(None, ALL), P(None, ALL)),
        check_vma=False,
    )
```

```python
import functools
import operator

import jax
import jax.numpy as jnp
from jax import lax
from jax.experimental import pallas as pl
from jax.experimental.pallas import tpu as pltpu
from jax.sharding import PartitionSpec as P


noise_var = 0.5
ALL = ("rows", "cols")
LANES = 128
UNIT = 4
PACK = 16
CHUNK = 512
WIDE = 256
LOG2_E = 1.4426950408889634
GRANT = 8 << 20


def exchange(value, mask):
    count = lax.axis_size(ALL)
    return lax.ppermute(value, ALL, [(i, i ^ mask) for i in range(count)])


def mask_groups():
    count = lax.axis_size(ALL)
    bits = [1 << k for k in range(1, count.bit_length() - 1)]
    return [bits[k : k + 2] for k in range(0, len(bits), 2)]


def scalar(table_ref, row):
    return table_ref[row][0, 0]


def choose_kernel(step_no, masks, table_ref, *refs):
    *options, out_ref = refs
    near = scalar(table_ref, 1 + step_no) & functools.reduce(operator.or_, masks)
    for mask, option_ref in zip(masks, options):

        @pl.when(near == mask)
        def _():
            out_ref[...] = option_ref[...]


def spread_step(mine, other, step_no, table):
    def choose(masks, options):
        (chosen,) = call(
            functools.partial(choose_kernel, step_no, tuple(masks)),
            [on_chip(mine.shape, mine.dtype)],
            [],
            placed_on_chip([table, *options]),
            [],
            1 << 10,
        )
        return chosen

    held = choose([0, 1], [mine, exchange(other, 1)])
    groups = mask_groups()
    for bits in groups:
        masks = [bits[0]] if len(bits) == 1 else [bits[0], bits[1], bits[0] | bits[1]]
        arrived = []
        for mask in masks:
            arrived.append(exchange(held, mask))
        held = choose([0, *masks], [held, *arrived])
    return held, exchange(held, 1)


def split3(value):
    high = value.astype(jnp.bfloat16)
    rest = value - high.astype(jnp.float32)
    middle = rest.astype(jnp.bfloat16)
    low = (rest - middle.astype(jnp.float32)).astype(jnp.bfloat16)
    return high, middle, low


def norm_rows(value, first):
    half = (-0.5 * LOG2_E) * jnp.sum(value * value, axis=0, keepdims=True)
    row = lax.broadcasted_iota(jnp.int32, (PACK, value.shape[1]), 0)
    block = jnp.where(row < 6, 1.0, 0.0)
    for k, part in enumerate(split3(half)):
        block = jnp.where(row == first + k, part.astype(jnp.float32), block)
    return block.astype(jnp.bfloat16)


def pack_left(value):
    high, middle, low = split3(value * LOG2_E)
    rows = [high, high, middle, high, low, middle, norm_rows(value, 0), jnp.zeros_like(high)]
    return jnp.concatenate(rows, axis=0)


def pack_right(value):
    high, middle, low = split3(value)
    rows = [high, middle, high, low, high, middle, norm_rows(value, 3), jnp.zeros_like(high)]
    return jnp.concatenate(rows, axis=0)


def kernel_values(left, right):
    exponent = jnp.dot(left, right, preferred_element_type=jnp.float32)
    return jnp.exp2(exponent).astype(jnp.bfloat16)


def units_of(rows, columns):
    return [(r, c) for r in range(0, rows, UNIT) for c in range(0, columns, LANES)]


def pick_kernel(
    per_anchor, device_ref, owners_ref, slots_ref, index_ref, points_ref, scale_ref, out_ref,
    scaled_ref, table_ref,
):
    dims, points = points_ref.shape
    device = device_ref[0]
    steps = owners_ref.shape[0]
    table_ref[0] = jnp.full(table_ref.shape[1:], device, jnp.int32)
    for k in range(steps):
        table_ref[1 + k] = jnp.full(table_ref.shape[1:], device ^ owners_ref[k], jnp.int32)
        table_ref[1 + steps + k] = jnp.full(table_ref.shape[1:], slots_ref[k], jnp.int32)
    same = lax.broadcasted_iota(jnp.int32, (dims, dims), 0) == lax.broadcasted_iota(
        jnp.int32, (dims, dims), 1
    )
    scale = jnp.sum(jnp.where(same, scale_ref[...], 0.0), axis=1, keepdims=True)
    scaled = points_ref[...] / scale
    scaled_ref[...] = scaled
    count, per = out_ref.shape[:2]
    per_block = per - per_anchor
    anchors = index_ref.shape[1]
    anchor_units, block_units = units_of(dims, anchors), units_of(dims, points)
    if len(anchor_units) < count * per_anchor or len(block_units) < count * per_block:
        out_ref[...] = jnp.zeros_like(out_ref)
    for i, (r, c) in enumerate(block_units):
        out_ref[i // per_block, per_anchor + i % per_block] = scaled[r : r + UNIT, c : c + LANES]
    parts = jnp.concatenate(split3(scaled), axis=0)
    width = min(WIDE, anchors)
    place = {spot: i for i, spot in enumerate(anchor_units)}
    for start in range(0, anchors, width):
        local = index_ref[:, start : start + width] - device * points
        hot = lax.broadcasted_iota(jnp.int32, (points, width), 0) == local
        got = jnp.dot(parts, hot.astype(jnp.bfloat16), preferred_element_type=jnp.float32)
        got = (got[:dims] + got[dims : 2 * dims]) + got[2 * dims :]
        for r in range(0, dims, UNIT):
            for c in range(0, width, LANES):
                i = place[r, start + c]
                out_ref[i // per_anchor, i % per_anchor] = got[r : r + UNIT, c : c + LANES]


def merge_kernel(per_anchor, steps, table_ref, got_ref, *refs):
    out_ref = refs[-1]
    count, per = got_ref.shape[:2]
    per_block = per - per_anchor
    device = scalar(table_ref, 0)
    total = got_ref[0, :per_anchor]
    for source in range(1, count):
        total = total + got_ref[source, :per_anchor]
    pieces = [total]
    for k in range(steps):
        owner = scalar(table_ref, 1 + k) ^ device
        pieces.append(got_ref[owner, per_anchor : per_anchor + per_block])
    piece = jnp.concatenate(pieces, axis=0)
    for target in range(count):
        out_ref[target] = piece


def gather_units(got_ref, first, per, whole_ref):
    for i, (r, c) in enumerate(units_of(*whole_ref.shape)):
        whole_ref[r : r + UNIT, c : c + LANES] = got_ref[i // per, first + i % per]


def project(residual, slot, core, inverse_ref, whole_ref, mine_ref, other_ref):
    inverse = inverse_ref[slot]
    product = jnp.dot(residual.astype(jnp.bfloat16), inverse, preferred_element_type=jnp.float32)
    whole_ref[...] = product.astype(jnp.bfloat16)
    half = mine_ref.shape[0]
    mine_ref[...] = whole_ref[pl.ds(pl.multiple_of(core * half, half), half)]
    other_ref[...] = whole_ref[pl.ds(pl.multiple_of((1 - core) * half, half), half)]


def warm_kernel(per_anchor, steps, table_ref, got_ref, scaled_ref, inverse_ref, *refs):
    *shares, aim_ref = refs[:-9]
    out_ref, mine_ref, other_ref, anchors_ref, left_ref, whole_ref = refs[-9:-3]
    share_ref, targets_ref, sems = refs[-3:]
    fetches = [pltpu.make_async_copy(aim_ref, targets_ref, sems.at[len(shares)])]
    for i, ref in enumerate(shares):
        fetches.append(pltpu.make_async_copy(ref, share_ref.at[i], sems.at[i]))
    for fetch in fetches:
        fetch.start()
    device = scalar(table_ref, 0)
    gather_units(got_ref, 0, per_anchor, anchors_ref)
    left_ref[...] = pack_left(anchors_ref[...]).T
    right = pack_right(scaled_ref[...])
    column = lax.rem(device, len(shares))
    for fetch in fetches:
        fetch.wait()
    share = share_ref.shape[2]
    step = min(CHUNK, share)
    for c in range(0, right.shape[1], WIDE):
        total = jnp.zeros((out_ref.shape[0], WIDE), jnp.float32)
        for mask in range(len(shares)):
            origin = (column ^ mask) * share
            for start in range(0, share, step):
                left = left_ref[pl.ds(pl.multiple_of(origin + start, LANES), step)]
                total = total + jnp.dot(
                    share_ref[mask, :, start : start + step],
                    kernel_values(left, right[:, c : c + WIDE]),
                    preferred_element_type=jnp.float32,
                )
        out_ref[:, c : c + WIDE] = targets_ref[:, c : c + WIDE] - total
    project(out_ref[...], scalar(table_ref, 1 + steps), device & 1, inverse_ref, whole_ref, mine_ref, other_ref)


def tile_kernel(first, per_block, got_ref, scaled_ref, out_ref, block_ref, left_ref):
    gather_units(got_ref, first, per_block, block_ref)
    left_ref[...] = pack_left(block_ref[...]).T
    right = pack_right(scaled_ref[...])
    for r in range(0, out_ref.shape[0], WIDE):
        for c in range(0, out_ref.shape[1], WIDE):
            out_ref[r : r + WIDE, c : c + WIDE] = kernel_values(
                left_ref[r : r + WIDE], right[:, c : c + WIDE]
            )


def update_kernel(step_no, steps, table_ref, held_ref, partner_ref, tile_ref, *refs):
    half = held_ref.shape[0]
    device = scalar(table_ref, 0)
    core = device & 1
    refs = list(refs)
    residual_ref = refs.pop(0)
    weights_ref = refs.pop(0) if step_no else None
    inverse_ref = refs.pop(0) if step_no < steps - 1 else None
    out_ref, sum_ref, *halves, whole_ref = refs
    whole_ref[pl.ds(pl.multiple_of(core * half, half), half)] = held_ref[...]
    whole_ref[pl.ds(pl.multiple_of((1 - core) * half, half), half)] = partner_ref[...]
    delta = whole_ref[...]
    residual = residual_ref[...] - jnp.dot(
        delta, tile_ref[...], preferred_element_type=jnp.float32
    )
    owned = jnp.where(scalar(table_ref, 1 + step_no) == 0, delta.astype(jnp.float32), 0.0)
    residual = residual - noise_var * owned
    out_ref[...] = residual
    sum_ref[...] = weights_ref[...] + owned if step_no else owned
    if step_no < steps - 1:
        slot = scalar(table_ref, 2 + steps + step_no)
        project(residual, slot, core, inverse_ref, whole_ref, *halves)


def on_chip(shape, dtype):
    return pltpu.VMEM(shape, dtype)


def call(kernel, out_shape, scalars, arrays, scratch, flops, outside=()):
    memory = [pltpu.SMEM] * len(scalars) + [pltpu.VMEM] * len(arrays) + [pltpu.HBM] * len(outside)
    return pl.pallas_call(
        kernel,
        out_shape=out_shape,
        in_specs=[pl.BlockSpec(memory_space=space) for space in memory],
        out_specs=[pl.BlockSpec(memory_space=pltpu.VMEM) for _ in out_shape],
        scratch_shapes=scratch,
        cost_estimate=pl.CostEstimate(flops=flops, transcendentals=0, bytes_accessed=1 << 20),
        compiler_params=pltpu.CompilerParams(vmem_limit_bytes=GRANT),
    )(*scalars, *arrays, *[pltpu.with_memory_space_constraint(x, pltpu.HBM) for x in outside])


def in_memory(arrays):
    return [pltpu.with_memory_space_constraint(array, pltpu.HBM) for array in arrays]


def placed_on_chip(arrays):
    return [pltpu.with_memory_space_constraint(array, pltpu.VMEM) for array in arrays]


def body(
    points, lengthscales, targets, inducing_weights, inducing_index, block_order, block_inverse
):
    dims, points_dev = points.shape
    per_device = block_inverse.shape[0]
    step_count = block_order.shape[0]
    anchor_count = inducing_index.shape[0]
    count, col_count = lax.axis_size(ALL), lax.axis_size("cols")
    device = lax.axis_index(ALL).reshape(1)
    owners = block_order // per_device
    slots = block_order % per_device
    others = [
        lax.ppermute(inducing_weights, "cols", [(i, i ^ mask) for i in range(col_count)])
        for mask in range(1, col_count)
    ]
    per_anchor = -(-len(units_of(dims, anchor_count)) // count)
    per_block = -(-len(units_of(dims, points_dev)) // count)
    tile_flops = 2 * LANES * points_dev
    half = (targets.shape[0] // 2, points_dev)
    halves = [on_chip(half, jnp.bfloat16)] * 2
    out, scaled, table = call(
        functools.partial(pick_kernel, per_anchor),
        [
            on_chip((count, per_anchor + per_block, UNIT, LANES), jnp.float32),
            on_chip(points.shape, jnp.float32),
            on_chip((1 + 2 * step_count, 8, LANES), jnp.int32),
        ],
        in_memory([device, owners, slots]),
        in_memory([inducing_index[None, :], points, lengthscales[None, :]]),
        [],
        2 * 3 * dims * points_dev * anchor_count,
    )
    got = lax.all_to_all(out, ALL, 0, 0)
    (copies,) = call(
        functools.partial(merge_kernel, per_anchor, step_count),
        [
            on_chip((count, per_anchor + step_count * per_block, UNIT, LANES), jnp.float32),
        ],
        [],
        placed_on_chip([table, got]),
        [],
        1 << 20,
        others,
    )
    shared = lax.all_to_all(copies, ALL, 0, 0)
    residual, mine, other = call(
        functools.partial(warm_kernel, per_anchor, step_count),
        [on_chip(targets.shape, jnp.float32), *halves],
        [],
        placed_on_chip([table, shared, scaled, block_inverse]),
        [
            pltpu.VMEM((dims, anchor_count), jnp.float32),
            pltpu.VMEM((anchor_count, LANES), jnp.bfloat16),
            pltpu.VMEM(targets.shape, jnp.bfloat16),
            pltpu.VMEM((col_count, *inducing_weights.shape), jnp.bfloat16),
            pltpu.VMEM(targets.shape, jnp.float32),
            pltpu.SemaphoreType.DMA((col_count + 1,)),
        ],
        tile_flops * anchor_count,
        [inducing_weights, *others, targets],
    )
    weights = None
    for step_no in range(step_count):
        last = step_no == step_count - 1
        held, partner = spread_step(mine, other, step_no, table)
        (tile,) = call(
            functools.partial(tile_kernel, per_anchor + step_no * per_block, per_block),
            [on_chip((points_dev, points_dev), jnp.bfloat16)],
            [],
            placed_on_chip([shared, scaled]),
            [pltpu.VMEM(points.shape, jnp.float32), pltpu.VMEM((points_dev, LANES), jnp.bfloat16)],
            tile_flops * points_dev,
        )
        state = [table, held, partner, tile, residual]
        if step_no:
            state.append(weights)
        if not last:
            state.append(block_inverse)
        shape = jax.ShapeDtypeStruct if last else on_chip
        results = call(
            functools.partial(update_kernel, step_no, step_count),
            [shape(targets.shape, jnp.float32)] * 2 + ([] if last else halves),
            [],
            placed_on_chip(state),
            [pltpu.VMEM(targets.shape, jnp.bfloat16)],
            tile_flops * points_dev // 4,
        )
        residual, weights, *rest = results
        if not last:
            mine, other = rest
    return (residual, weights)


def solution(mesh):
    placed = (
        P(None, ALL),
        P(),
        P(None, ALL),
        P(None, "cols"),
        P(),
        P(),
        P(ALL, None, None),
    )

    return jax.shard_map(
        body,
        mesh=mesh,
        in_specs=placed,
        out_specs=(P(None, ALL), P(None, ALL)),
        check_vma=False,
    )
```
